32 devices in a mesh: img: 8 (over y, x, core), head: 4 (over z).
Axes of the slice: x: 2, y: 2, z: 4, core: 2. Of those that a mesh axis runs over, the one named last changes fastest.
Arguments:
- latent_init: bfloat16 [64, 1024], replicated, may hold values from -6 to 6
- media: bfloat16 [16, 256, 1024], P('img'), may hold values from -6 to 6
- patch_counts: int32 [16], P('img'), may hold values from 64 to 256, as said below
- query_weight: bfloat16 [2, 1024, 1024], P(None, None, 'head'), may hold values from -0.1875 to 0.1875
- key_weight: bfloat16 [2, 1024, 1024], P(None, None, 'head'), may hold values from -0.1875 to 0.1875
- value_weight: bfloat16 [2, 1024, 1024], P(None, None, 'head'), may hold values from -0.1875 to 0.1875
- w_out: bfloat16 [2, 1024, 1024], P(None, 'head'), may hold values from -1.5 to 1.5
- up_weight: bfloat16 [2, 1024, 4096], P(None, None, 'head'), may hold values from -0.1875 to 0.1875
- w_down: bfloat16 [2, 4096, 1024], P(None, 'head'), may hold values from -0.09375 to 0.09375
- ln_gain: float32 [2, 3, 1024], replicated, may hold values from 0.5 to 1.5
- ln_bias: float32 [2, 3, 1024], replicated, may hold values from -1.75 to 1.75
- latent_cot: bfloat16 [16, 64, 1024], P('img'), may hold values from -6 to 6
Outputs:
- latents_out: bfloat16 [16, 64, 1024], P('img')
- media_grad: float32 [16, 256, 1024], P('img')
- latent_init_grad: float32 [64, 1024], replicated
- grad_w_query: float32 [2, 1024, 1024], P(None, None, 'head')
- grad_w_key: float32 [2, 1024, 1024], P(None, None, 'head')
- grad_w_value: float32 [2, 1024, 1024], P(None, None, 'head')
- grad_w_out: float32 [2, 1024, 1024], P(None, 'head')
- grad_w_up: float32 [2, 1024, 4096], P(None, None, 'head')
- grad_w_down: float32 [2, 4096, 1024], P(None, 'head')
- grad_ln_gain: float32 [2, 3, 1024], replicated
- grad_ln_bias: float32 [2, 3, 1024], replicated
The draws below stay inside these ranges and needn't reach their ends.
Inputs may be any that keep to these rules, and one draw needn't show every extreme that they name: `patch_counts`: an image's valid patches are its first ones; in every draw some image has all 256 patches valid.
All inputs are finite; a program needn't handle non-finite values.
Results may differ from the reference program's by a relative error of at most 0.017.
Values sent between devices are 32-bit elements; how exact they have to be, the bound alone decides.
No kernel may reach another device: no remote copies, remote signals or barrier semaphores. Data moves between devices by JAX's collectives and lax.ppermute only.
A program may use at most 192 MiB of HBM per device.

```python
import jax
import jax.numpy as jnp
from jax import lax

D = 1024
HEADS = 16
HEAD_DIM = 64
LAT = 64
FF = 4096
PATCHES = 256
LAYERS = 2
IMAGES = 16


def draw_patch_counts(key, part):
    counts = jax.random.randint(key, (IMAGES,), PATCHES // 4, PATCHES + 1, dtype=jnp.int32)
    chosen = jax.random.randint(jax.random.fold_in(key, 7), (), 0, IMAGES, dtype=jnp.int32)
    return jnp.where(jnp.arange(IMAGES, dtype=jnp.int32) == chosen, PATCHES, counts).astype(jnp.int32)


def block_scale(rng, extent, split, low, high):
    def one(position, blocks):
        steps = jax.random.uniform(jax.random.fold_in(jax.random.fold_in(rng, 6), position), (blocks,), jnp.float32, low / len(split), high / len(split))
        return jnp.repeat(jnp.exp(steps), extent[position] // blocks).reshape((-1,) + (1,) * (len(extent) - position - 1))

    gain = one(*split[0])
    for cut in split[1:]:
        gain = gain * one(*cut)
    return gain


def normal_values(stream_key, extent, deviation, bound, split=(), kind=jnp.bfloat16):
    array = jax.random.normal(stream_key, extent, jnp.float32) * deviation
    if len(split) > 0:
        array = block_scale(stream_key, extent, split, -0.22, 0.18) * array
    return jnp.clip(array, min=-bound, max=bound).astype(kind)


def setup_inputs(seed: int = 0) -> dict:
    key_list = jax.random.split(jax.random.key(seed), 13)
    latent_init = normal_values(key_list[0], (LAT, D), 1.0, 6.0)
    media = normal_values(key_list[1], (IMAGES, PATCHES, D), 1.0, 6.0, ((0, 8),))
    patch_counts = draw_patch_counts(jax.random.fold_in(key_list[12], 71), 0)
    query_weight = normal_values(key_list[3], (LAYERS, D, D), D ** -0.5, 0.1875, ((2, 4),))
    key_weight = normal_values(key_list[4], (LAYERS, D, D), D ** -0.5, 0.1875, ((2, 4),))
    value_weight = normal_values(key_list[5], (LAYERS, D, D), D ** -0.5, 0.1875, ((2, 4),))
    w_out = normal_values(key_list[6], (LAYERS, D, D), HEADS ** -0.5, 1.5, ((1, 4),))
    up_weight = normal_values(key_list[7], (LAYERS, D, FF), D ** -0.5, 0.1875, ((2, 4),))
    w_down = normal_values(key_list[8], (LAYERS, FF, D), FF ** -0.5, 0.09375, ((1, 4),))
    ln_gain = jnp.clip(1.0 + 0.1 * jax.random.normal(key_list[9], (LAYERS, 3, D), jnp.float32), 0.5, 1.5)
    ln_bias = normal_values(key_list[10], (LAYERS, 3, D), 0.3, 1.75, (), jnp.float32)
    latent_cot = normal_values(key_list[11], (IMAGES, LAT, D), 1.0, 6.0, ((0, 8),))
    return dict(latent_init=latent_init, media=media, patch_counts=patch_counts, query_weight=query_weight, key_weight=key_weight, value_weight=value_weight, w_out=w_out, up_weight=up_weight, w_down=w_down, ln_gain=ln_gain, ln_bias=ln_bias, latent_cot=latent_cot)


@jax.custom_vjp
def low(v):
    return lax.optimization_barrier(v.astype(jnp.bfloat16)).astype(jnp.float32)

@jax.custom_vjp
def low_back(v):
    return v

def low_keep(v):
    return (low(v), None)

def low_pass(kept, grad):
    return (grad,)

def back_keep(v):
    return (v, None)

def back_low(kept, grad):
    return (low(grad),)
low.defvjp(low_keep, low_pass)
low_back.defvjp(back_keep, back_low)

def layer_norm(values, gain_row, bias_row):
    center = values - lax.optimization_barrier(jnp.mean(values, axis=-1, keepdims=True))
    variance = lax.optimization_barrier(jnp.mean(center * center, axis=-1, keepdims=True))
    return center * lax.rsqrt(variance + 1e-05) * gain_row + bias_row

def project(values, matrix):
    return jnp.einsum('brd,de->bre', values, matrix, precision=lax.Precision.HIGHEST)

def forward(latent_init, media, query_weight, key_weight, value_weight, w_out, up_weight, w_down, ln_gain, ln_bias, key_valid):
    count_img = media.shape[0]
    latent = jnp.broadcast_to(latent_init[None], (count_img, LAT, D))
    for layer_position in range(LAYERS):
        norm_media = low(layer_norm(media, ln_gain[layer_position, 0], ln_bias[layer_position, 0]))
        latent_normed = low(layer_norm(latent, ln_gain[layer_position, 1], ln_bias[layer_position, 1]))
        joined_rows = jnp.concatenate([norm_media, latent_normed], axis=1)
        query_rows = low(low_back(project(latent_normed, query_weight[layer_position])))
        key_results = low(low_back(project(joined_rows, key_weight[layer_position])))
        value_results = low(low_back(project(joined_rows, value_weight[layer_position])))
        query_heads = query_rows.reshape(count_img, LAT, HEADS, HEAD_DIM)
        key_heads = key_results.reshape(count_img, PATCHES + LAT, HEADS, HEAD_DIM)
        value_heads = value_results.reshape(count_img, PATCHES + LAT, HEADS, HEAD_DIM)
        scores = jnp.einsum('bqhd,bkhd->bhqk', query_heads, key_heads, precision=lax.Precision.HIGHEST) * HEAD_DIM ** (-0.5)
        scores = low_back(scores)
        scores = jnp.where(key_valid[:, None, None, :], scores, -1e+30)
        weights_soft = jax.nn.softmax(scores, axis=-1)
        mixed = jnp.einsum('bhqk,bkhd->bqhd', low(weights_soft), value_heads, precision=lax.Precision.HIGHEST)
        mixed = low(low_back(mixed.reshape(count_img, LAT, D)))
        hidden = latent + low_back(project(mixed, w_out[layer_position]))
        hidden_normed = low(layer_norm(hidden, ln_gain[layer_position, 2], ln_bias[layer_position, 2]))
        up_results = low_back(project(hidden_normed, up_weight[layer_position]))
        active = low(jax.nn.gelu(up_results, approximate=False))
        latent = hidden + low_back(project(active, w_down[layer_position]))
    return latent

def reference(latent_init, media, patch_counts, query_weight, key_weight, value_weight, w_out, up_weight, w_down, ln_gain, ln_bias, latent_cot):
    count_img = media.shape[0]
    places = jnp.arange(PATCHES, dtype=jnp.int32)
    key_valid = jnp.concatenate([places[None, :] < patch_counts[:, None], jnp.ones((count_img, LAT), dtype=bool)], axis=1)

    def closed(init_full, media_full, query_full, key_full, value_full, out_full, up_full, down_full, gain_full, bias_full):
        return forward(init_full, media_full, query_full, key_full, value_full, out_full, up_full, down_full, gain_full, bias_full, key_valid)
    result, pullback = jax.vjp(closed, latent_init.astype(jnp.float32), media.astype(jnp.float32), query_weight.astype(jnp.float32), key_weight.astype(jnp.float32), value_weight.astype(jnp.float32), w_out.astype(jnp.float32), up_weight.astype(jnp.float32), w_down.astype(jnp.float32), ln_gain, ln_bias)
    grads = pullback(latent_cot.astype(jnp.float32))
    return (result.astype(jnp.bfloat16), grads[1], grads[0], grads[2], grads[3], grads[4], grads[5], grads[6], grads[7], grads[8], grads[9])
```

```python
import jax
import jax.numpy as jnp
from jax import lax
from jax.sharding import PartitionSpec as P

HEAD_DIM = 64
F32 = jnp.float32
BF16 = jnp.bfloat16


def mm(form, left, right):
    return jnp.einsum(form, left, right, preferred_element_type=F32)


def norm_parts(values):
    center = values - jnp.mean(values, axis=-1, keepdims=True)
    rstd = lax.rsqrt(jnp.mean(center * center, axis=-1, keepdims=True) + 1e-05)
    return center * rstd, rstd


def norm_back(dn, zhat, rstd, gain):
    e = dn * gain
    return (
        e - jnp.mean(e, axis=-1, keepdims=True) - zhat * jnp.mean(e * zhat, axis=-1, keepdims=True)
    ) * rstd


def make_body(heads_size, img_size):
    head_bits = [1 << k for k in range(heads_size.bit_length() - 1)]
    img_bits = [1 << k for k in range(1, img_size.bit_length() - 1)]

    def swap(x, axis, bit):
        size = heads_size if axis == "head" else img_size
        return lax.ppermute(x, axis, [(i, i ^ bit) for i in range(size)])

    def rows_of(x, start, size):
        return lax.dynamic_slice_in_dim(x, start, size, 0)

    def head_sum_half(part):
        half = part.shape[1] // 2
        kept = part[:, :half] + swap(part[:, half:], "head", 1)
        for bit in head_bits[1:]:
            kept = kept + swap(kept, "head", bit)
        return kept

    def head_fill(rows):
        return jnp.concatenate([rows, swap(rows, "head", 1)], axis=1)

    def orders():
        return img_bits, img_bits[::-1]

    def img_gather(rows):
        half = rows.shape[0] // 2
        parts = [rows[:half], rows[half:]]
        first, second = orders()
        for one, two in zip(first, second):
            parts = [
                jnp.concatenate([parts[0], swap(parts[0], "img", one)], 0),
                jnp.concatenate([parts[1], swap(parts[1], "img", two)], 0),
            ]
        mine = jnp.concatenate(parts, 0)
        return jnp.concatenate([mine, swap(mine, "img", 1)], 0)

    def img_sum(total):
        place = lax.axis_index("img")

        def bit_of(bit):
            return (place // bit) % 2

        def split(x, bit):
            half = x.shape[0] // 2
            b = bit_of(bit)
            return rows_of(x, b * half, half) + swap(rows_of(x, (1 - b) * half, half), "img", bit)

        def join(x, bit):
            other = swap(x, "img", bit)
            return jnp.where(
                bit_of(bit) == 0,
                jnp.concatenate([x, other], 0),
                jnp.concatenate([other, x], 0),
            )

        mine = split(total, 1)
        half = mine.shape[0] // 2
        parts = [mine[:half], mine[half:]]
        first, second = orders()
        for one, two in zip(first, second):
            parts = [split(parts[0], one), split(parts[1], two)]
        for one, two in zip(first[::-1], second[::-1]):
            parts = [join(parts[0], one), join(parts[1], two)]
        return join(jnp.concatenate(parts, 0), 1)

    def body(
        latent_init,
        media,
        patch_counts,
        query_weight,
        key_weight,
        value_weight,
        w_out,
        up_weight,
        w_down,
        ln_gain,
        ln_bias,
        latent_cot,
    ):
        images, patches, width = media.shape
        latents = latent_init.shape[0]
        layers = query_weight.shape[0]
        local = query_weight.shape[2]
        heads = local // HEAD_DIM
        half = latents // 2
        scale = HEAD_DIM ** (-0.5)
        share = 2.0 / heads_size
        odd = lax.axis_index("head") % 2
        one = jnp.where(patch_counts[0] >= 0, 1.0, 2.0).astype(F32)

        def turn(x, axis):
            first, second = jnp.split(x, 2, axis)
            return jnp.where(
                odd == 0,
                jnp.concatenate([first, second], axis),
                jnp.concatenate([second, first], axis),
            )

        start = turn(latent_init, 0).astype(F32)
        cot = turn(latent_cot, 1).astype(F32)
        media_z, media_rstd = norm_parts(media.astype(F32))
        places = jnp.arange(patches + latents, dtype=jnp.int32)
        valid = (places[None, :] < patch_counts[:, None]) | (places[None, :] >= patches)

        def attend(latent_z, layer):
            norm_media = (media_z * ln_gain[layer, 0] + ln_bias[layer, 0]).astype(BF16)
            normed = (latent_z * ln_gain[layer, 1] + ln_bias[layer, 1]).astype(BF16)
            joined = jnp.concatenate([norm_media, normed], axis=1)
            q = mm("brd,de->bre", normed, query_weight[layer]).astype(BF16)
            k = mm("brd,de->bre", joined, key_weight[layer]).astype(BF16)
            v = mm("brd,de->bre", joined, value_weight[layer]).astype(BF16)
            qh = q.reshape(images, latents, heads, HEAD_DIM)
            kh = k.reshape(images, patches + latents, heads, HEAD_DIM)
            vh = v.reshape(images, patches + latents, heads, HEAD_DIM)
            scores = mm("bqhd,bkhd->bhqk", qh, kh) * scale
            scores = jnp.where(valid[:, None, None, :], scores, -1e30)
            probs = jax.nn.softmax(scores, axis=-1)
            low = probs.astype(BF16)
            mixed = mm("bhqk,bkhd->bqhd", low, vh).reshape(images, latents, local).astype(BF16)
            out = mm("bqe,ef->bqf", mixed, w_out[layer])
            return dict(
                normed=normed, joined=joined, qh=qh, kh=kh, vh=vh, probs=probs, low=low,
                mixed=mixed,
            ), out

        def hidden_norm(zhat, layer):
            return (zhat * ln_gain[layer, 2] + ln_bias[layer, 2]).astype(BF16)

        resid = jnp.broadcast_to(start[None, :half], (images, half, width))
        start_z, start_rstd = norm_parts(start)
        latent_z = jnp.broadcast_to(start_z[None], (images, latents, width))
        latent_stat = [None] * layers
        latent_zs = [None] * layers
        hidden_stat = [None] * layers
        hidden_zs = [None] * layers
        kept = [None] * layers
        ups = [None] * layers
        latent_stat[0] = None
        for layer in range(layers):
            latent_zs[layer] = latent_z
            kept[layer], out = attend(latent_z, layer)
            hid = resid + head_sum_half(out)
            z_half, rstd = norm_parts(hid)
            hidden_stat[layer] = (z_half, rstd)
            hidden_zs[layer] = head_fill(z_half)
            up = mm("brd,de->bre", hidden_norm(hidden_zs[layer], layer), up_weight[layer])
            ups[layer] = up
            active = jax.nn.gelu(up, approximate=False).astype(BF16)
            down = mm("bre,ed->brd", active, w_down[layer])
            resid = hid + head_sum_half(down)
            if layer + 1 < layers:
                z_half, rstd = norm_parts(resid)
                latent_stat[layer + 1] = (z_half, rstd)
                latent_z = head_fill(z_half)
        latents_out = turn(head_fill(resid) * one, 1).astype(BF16)

        grad_full = cot
        grad = cot[:, :half]
        gain_rows = [[None] * 3 for _ in range(layers)]
        bias_rows = [[None] * 3 for _ in range(layers)]
        media_part = 0.0
        attn_grads = [None] * layers
        up_grads = [None] * layers
        down_grads = [None] * layers
        for layer in reversed(range(layers)):
            c = kept[layer]
            dy = (grad_full * one).astype(BF16)
            dact = mm("brd,ed->bre", dy, w_down[layer])
            _, pull = jax.vjp(lambda t: jax.nn.gelu(t, approximate=False), ups[layer])
            dup = pull(dact)[0].astype(BF16)
            dhn = head_sum_half(mm("bre,de->brd", dup, up_weight[layer]))
            z_half, rstd = hidden_stat[layer]
            gain_rows[layer][2] = jnp.sum(dhn * z_half, (0, 1)) * share
            bias_rows[layer][2] = jnp.sum(dhn, (0, 1)) * share
            dhid = grad + norm_back(dhn, z_half, rstd, ln_gain[layer, 2])
            all_z = img_gather(hidden_zs[layer].reshape(images * latents, width))
            all_dy = (img_gather(grad_full.reshape(images * latents, width)) * one).astype(BF16)
            all_hn = hidden_norm(all_z, layer)
            all_up = mm("rd,de->re", all_hn, up_weight[layer])
            all_act, pull = jax.vjp(lambda t: jax.nn.gelu(t, approximate=False), all_up)
            all_dup = pull(mm("rd,ed->re", all_dy, w_down[layer]))[0].astype(BF16)
            down_grads[layer] = mm("re,rd->ed", all_act.astype(BF16), all_dy)
            up_grads[layer] = mm("rd,re->de", all_hn, all_dup)
            dlow = (head_fill(dhid) * one).astype(BF16)
            grad_wo = mm("brd,bre->de", dlow, c["mixed"])
            dmix = mm("brd,ed->bre", dlow, w_out[layer]).astype(BF16)
            dmh = dmix.reshape(c["qh"].shape)
            dprob = mm("bqhd,bkhd->bhqk", dmh, c["vh"])
            dv = mm("bhqk,bqhd->bkhd", c["low"], dmh).astype(BF16)
            total = jnp.sum(dprob * c["probs"], axis=-1, keepdims=True)
            dscore = (c["probs"] * (dprob - total)).astype(BF16)
            dq = (mm("bhqk,bkhd->bqhd", dscore, c["kh"]) * scale).astype(BF16)
            dk = (mm("bhqk,bqhd->bkhd", dscore, c["qh"]) * scale).astype(BF16)
            dq = dq.reshape(images, latents, local)
            dk = dk.reshape(images, patches + latents, local)
            dv = dv.reshape(images, patches + latents, local)
            packed = jnp.concatenate(
                [
                    mm("brd,bre->de", c["normed"], dq),
                    mm("brd,bre->de", c["joined"], dk),
                    mm("brd,bre->de", c["joined"], dv),
                    grad_wo,
                ],
                axis=1,
            )
            attn_grads[layer] = img_sum(packed)
            djoin = mm("bre,de->brd", dk, key_weight[layer]) + mm(
                "bre,de->brd", dv, value_weight[layer]
            )
            dmedia = djoin[:, :patches]
            dlat = djoin[:, patches:] + mm("bre,de->brd", dq, query_weight[layer])
            media_part = media_part + norm_back(dmedia, media_z, media_rstd, ln_gain[layer, 0])
            gain_rows[layer][0] = jnp.sum(dmedia * media_z, (0, 1))
            bias_rows[layer][0] = jnp.sum(dmedia, (0, 1))
            if layer > 0:
                dlat = head_sum_half(dlat)
                z_half, rstd = latent_stat[layer]
                gain_rows[layer][1] = jnp.sum(dlat * z_half, (0, 1)) * share
                bias_rows[layer][1] = jnp.sum(dlat, (0, 1)) * share
                grad = dhid + norm_back(dlat, z_half, rstd, ln_gain[layer, 1])
                grad_full = head_fill(grad)
            else:
                gain_rows[layer][1] = jnp.sum(dlat * start_z, (0, 1))
                bias_rows[layer][1] = jnp.sum(dlat, (0, 1))
                init_part = jnp.sum(
                    norm_back(dlat, start_z, start_rstd, ln_gain[layer, 1]), axis=0
                )
                init_half = jnp.sum(dhid, axis=0) * share

        media_grad = media_part
        rows = patches // 2
        own = lax.dynamic_slice_in_dim(media_part, odd * rows, rows, 1)
        rest = lax.dynamic_slice_in_dim(media_part, (1 - odd) * rows, rows, 1)
        media_grad = turn(head_fill(head_sum_half(jnp.concatenate([own, rest], 1))), 1)

        stats = jnp.stack([r for rr in gain_rows for r in rr] + [r for rr in bias_rows for r in rr])
        stats = jnp.pad(stats, ((0, -stats.shape[0] % 8), (0, 0)))
        stats = stats + swap(stats, "head", 1)
        init = init_part[:half] + swap(init_part[half:], "head", 1) + init_half
        pack = jnp.concatenate([init, stats], 0)
        for bit in head_bits[1:]:
            pack = pack + swap(pack, "head", bit)
        for bit in [1] + img_bits:
            pack = pack + swap(pack, "img", bit)
        init = turn(jnp.concatenate([pack[:half], swap(pack[:half], "head", 1)], 0), 0)
        count = layers * 3
        grad_gain = pack[half : half + count].reshape(layers, 3, width)
        grad_bias = pack[half + count : half + 2 * count].reshape(layers, 3, width)

        def piece(j):
            return jnp.stack([g[:, j * local : (j + 1) * local] for g in attn_grads])

        return (
            latents_out,
            media_grad,
            init,
            piece(0),
            piece(1),
            piece(2),
            jnp.stack([g[:, 3 * local :].T for g in attn_grads]),
            jnp.stack(up_grads),
            jnp.stack(down_grads),
            grad_gain,
            grad_bias,
        )

    return body


def solution(mesh):
    in_specs = (
        P(),
        P("img", None, None),
        P("img"),
        P(None, None, "head"),
        P(None, None, "head"),
        P(None, None, "head"),
        P(None, "head", None),
        P(None, None, "head"),
        P(None, "head", None),
        P(),
        P(),
        P("img", None, None),
    )
    out_specs = (
        P("img", None, None),
        P("img", None, None),
        P(),
        P(None, None, "head"),
        P(None, None, "head"),
        P(None, None, "head"),
        P(None, "head", None),
        P(None, None, "head"),
        P(None, "head", None),
        P(),
        P(),
    )
    return jax.shard_map(
        make_body(mesh.shape["head"], mesh.shape["img"]),
        mesh=mesh,
        in_specs=in_specs,
        out_specs=out_specs,
        check_vma=False,
    )
```

```python
import jax
import jax.numpy as jnp
from jax import lax
from jax.experimental import pallas as pl
from jax.experimental.pallas import tpu as pltpu
from jax.sharding import PartitionSpec as P

HEAD_DIM = 64
F32 = jnp.float32
BF16 = jnp.bfloat16


def mm(form, left, right):
    return jnp.einsum(form, left, right, preferred_element_type=F32)


def norm_parts(values):
    center = values - jnp.mean(values, axis=-1, keepdims=True)
    rstd = lax.rsqrt(jnp.mean(center * center, axis=-1, keepdims=True) + 1e-05)
    return center * rstd, rstd


def norm_back(dn, zhat, rstd, gain):
    e = dn * gain
    return (
        e - jnp.mean(e, axis=-1, keepdims=True) - zhat * jnp.mean(e * zhat, axis=-1, keepdims=True)
    ) * rstd


def make_body(heads_size, img_size):
    head_bits = [1 << k for k in range(heads_size.bit_length() - 1)]
    img_bits = [1 << k for k in range(1, img_size.bit_length() - 1)]

    def swap(x, axis, bit):
        size = heads_size if axis == "head" else img_size
        return lax.ppermute(x, axis, [(i, i ^ bit) for i in range(size)])

    def rows_of(x, start, size):
        return lax.dynamic_slice_in_dim(x, start, size, 0)

    def head_sum_half(part):
        half = part.shape[1] // 2
        kept = part[:, :half] + swap(part[:, half:], "head", 1)
        for bit in head_bits[1:]:
            kept = kept + swap(kept, "head", bit)
        return kept

    def head_fill(rows):
        return jnp.concatenate([rows, swap(rows, "head", 1)], axis=1)

    def orders():
        return img_bits, img_bits[::-1]

    def img_gather(rows):
        half = rows.shape[0] // 2
        parts = [rows[:half], rows[half:]]
        first, second = orders()
        for one, two in zip(first, second):
            parts = [
                jnp.concatenate([parts[0], swap(parts[0], "img", one)], 0),
                jnp.concatenate([parts[1], swap(parts[1], "img", two)], 0),
            ]
        mine = jnp.concatenate(parts, 0)
        return jnp.concatenate([mine, swap(mine, "img", 1)], 0)

    def img_sum(total):
        place = lax.axis_index("img")

        def bit_of(bit):
            return (place // bit) % 2

        def split(x, bit):
            half = x.shape[0] // 2
            b = bit_of(bit)
            return rows_of(x, b * half, half) + swap(rows_of(x, (1 - b) * half, half), "img", bit)

        def join(x, bit):
            other = swap(x, "img", bit)
            return jnp.where(
                bit_of(bit) == 0,
                jnp.concatenate([x, other], 0),
                jnp.concatenate([other, x], 0),
            )

        mine = split(total, 1)
        half = mine.shape[0] // 2
        parts = [mine[:half], mine[half:]]
        first, second = orders()
        for one, two in zip(first, second):
            parts = [split(parts[0], one), split(parts[1], two)]
        for one, two in zip(first[::-1], second[::-1]):
            parts = [join(parts[0], one), join(parts[1], two)]
        return join(jnp.concatenate(parts, 0), 1)

    def body(
        latent_init,
        media,
        patch_counts,
        query_weight,
        key_weight,
        value_weight,
        w_out,
        up_weight,
        w_down,
        ln_gain,
        ln_bias,
        latent_cot,
    ):
        images, patches, width = media.shape
        latents = latent_init.shape[0]
        layers = query_weight.shape[0]
        local = query_weight.shape[2]
        heads = local // HEAD_DIM
        half = latents // 2
        scale = HEAD_DIM ** (-0.5)
        share = 2.0 / heads_size
        odd = lax.axis_index("head") % 2
        one = jnp.where(patch_counts[0] >= 0, 1.0, 2.0).astype(F32)

        def turn(x, axis):
            first, second = jnp.split(x, 2, axis)
            return jnp.where(
                odd == 0,
                jnp.concatenate([first, second], axis),
                jnp.concatenate([second, first], axis),
            )

        start = turn(latent_init, 0).astype(F32)
        cot = turn(latent_cot, 1).astype(F32)
        media_z, media_rstd = norm_parts(media.astype(F32))
        places = jnp.arange(patches + latents, dtype=jnp.int32)
        valid = (places[None, :] < patch_counts[:, None]) | (places[None, :] >= patches)

        def attend(latent_z, layer):
            norm_media = (media_z * ln_gain[layer, 0] + ln_bias[layer, 0]).astype(BF16)
            normed = (latent_z * ln_gain[layer, 1] + ln_bias[layer, 1]).astype(BF16)
            joined = jnp.concatenate([norm_media, normed], axis=1)
            q = mm("brd,de->bre", normed, query_weight[layer]).astype(BF16)
            k = mm("brd,de->bre", joined, key_weight[layer]).astype(BF16)
            v = mm("brd,de->bre", joined, value_weight[layer]).astype(BF16)
            qh = q.reshape(images, latents, heads, HEAD_DIM)
            kh = k.reshape(images, patches + latents, heads, HEAD_DIM)
            vh = v.reshape(images, patches + latents, heads, HEAD_DIM)
            scores = mm("bqhd,bkhd->bhqk", qh, kh) * scale
            scores = jnp.where(valid[:, None, None, :], scores, -1e30)
            probs = jax.nn.softmax(scores, axis=-1)
            low = probs.astype(BF16)
            mixed = mm("bhqk,bkhd->bqhd", low, vh).reshape(images, latents, local).astype(BF16)
            out = mm("bqe,ef->bqf", mixed, w_out[layer])
            return dict(
                normed=normed, joined=joined, qh=qh, kh=kh, vh=vh, probs=probs, low=low,
                mixed=mixed,
            ), out

        def hidden_norm(zhat, layer):
            return (zhat * ln_gain[layer, 2] + ln_bias[layer, 2]).astype(BF16)

        resid = jnp.broadcast_to(start[None, :half], (images, half, width))
        start_z, start_rstd = norm_parts(start)
        latent_z = jnp.broadcast_to(start_z[None], (images, latents, width))
        latent_stat = [None] * layers
        latent_zs = [None] * layers
        hidden_stat = [None] * layers
        hidden_zs = [None] * layers
        kept = [None] * layers
        ups = [None] * layers
        latent_stat[0] = None
        for layer in range(layers):
            latent_zs[layer] = latent_z
            kept[layer], out = attend(latent_z, layer)
            hid = resid + head_sum_half(out)
            z_half, rstd = norm_parts(hid)
            hidden_stat[layer] = (z_half, rstd)
            hidden_zs[layer] = head_fill(z_half)
            up = mm("brd,de->bre", hidden_norm(hidden_zs[layer], layer), up_weight[layer])
            ups[layer] = up
            active = jax.nn.gelu(up, approximate=False).astype(BF16)
            down = mm("bre,ed->brd", active, w_down[layer])
            resid = hid + head_sum_half(down)
            if layer + 1 < layers:
                z_half, rstd = norm_parts(resid)
                latent_stat[layer + 1] = (z_half, rstd)
                latent_z = head_fill(z_half)
        latents_out = turn(head_fill(resid) * one, 1).astype(BF16)

        grad_full = cot
        grad = cot[:, :half]
        gain_rows = [[None] * 3 for _ in range(layers)]
        bias_rows = [[None] * 3 for _ in range(layers)]
        media_part = 0.0
        attn_grads = [None] * layers
        up_grads = [None] * layers
        down_grads = [None] * layers
        for layer in reversed(range(layers)):
            c = kept[layer]
            dy = (grad_full * one).astype(BF16)
            dact = mm("brd,ed->bre", dy, w_down[layer])
            _, pull = jax.vjp(lambda t: jax.nn.gelu(t, approximate=False), ups[layer])
            dup = pull(dact)[0].astype(BF16)
            dhn = head_sum_half(mm("bre,de->brd", dup, up_weight[layer]))
            z_half, rstd = hidden_stat[layer]
            gain_rows[layer][2] = jnp.sum(dhn * z_half, (0, 1)) * share
            bias_rows[layer][2] = jnp.sum(dhn, (0, 1)) * share
            dhid = grad + norm_back(dhn, z_half, rstd, ln_gain[layer, 2])
            all_z = img_gather(hidden_zs[layer].reshape(images * latents, width))
            all_dy = (img_gather(grad_full.reshape(images * latents, width)) * one).astype(BF16)
            all_hn = hidden_norm(all_z, layer)
            all_up = mm("rd,de->re", all_hn, up_weight[layer])
            all_act, pull = jax.vjp(lambda t: jax.nn.gelu(t, approximate=False), all_up)
            all_dup = pull(mm("rd,ed->re", all_dy, w_down[layer]))[0].astype(BF16)
            down_grads[layer] = mm("re,rd->ed", all_act.astype(BF16), all_dy)
            up_grads[layer] = mm("rd,re->de", all_hn, all_dup)
            dlow = (head_fill(dhid) * one).astype(BF16)
            grad_wo = mm("brd,bre->de", dlow, c["mixed"])
            dmix = mm("brd,ed->bre", dlow, w_out[layer]).astype(BF16)
            dmh = dmix.reshape(c["qh"].shape)
            dprob = mm("bqhd,bkhd->bhqk", dmh, c["vh"])
            dv = mm("bhqk,bqhd->bkhd", c["low"], dmh).astype(BF16)
            total = jnp.sum(dprob * c["probs"], axis=-1, keepdims=True)
            dscore = (c["probs"] * (dprob - total)).astype(BF16)
            dq = (mm("bhqk,bkhd->bqhd", dscore, c["kh"]) * scale).astype(BF16)
            dk = (mm("bhqk,bqhd->bkhd", dscore, c["qh"]) * scale).astype(BF16)
            dq = dq.reshape(images, latents, local)
            dk = dk.reshape(images, patches + latents, local)
            dv = dv.reshape(images, patches + latents, local)
            packed = jnp.concatenate(
                [
                    mm("brd,bre->de", c["normed"], dq),
                    mm("brd,bre->de", c["joined"], dk),
                    mm("brd,bre->de", c["joined"], dv),
                    grad_wo,
                ],
                axis=1,
            )
            attn_grads[layer] = img_sum(packed)
            djoin = mm("bre,de->brd", dk, key_weight[layer]) + mm(
                "bre,de->brd", dv, value_weight[layer]
            )
            dmedia = djoin[:, :patches]
            dlat = djoin[:, patches:] + mm("bre,de->brd", dq, query_weight[layer])
            media_part = media_part + norm_back(dmedia, media_z, media_rstd, ln_gain[layer, 0])
            gain_rows[layer][0] = jnp.sum(dmedia * media_z, (0, 1))
            bias_rows[layer][0] = jnp.sum(dmedia, (0, 1))
            if layer > 0:
                dlat = head_sum_half(dlat)
                z_half, rstd = latent_stat[layer]
                gain_rows[layer][1] = jnp.sum(dlat * z_half, (0, 1)) * share
                bias_rows[layer][1] = jnp.sum(dlat, (0, 1)) * share
                grad = dhid + norm_back(dlat, z_half, rstd, ln_gain[layer, 1])
                grad_full = head_fill(grad)
            else:
                gain_rows[layer][1] = jnp.sum(dlat * start_z, (0, 1))
                bias_rows[layer][1] = jnp.sum(dlat, (0, 1))
                init_part = jnp.sum(
                    norm_back(dlat, start_z, start_rstd, ln_gain[layer, 1]), axis=0
                )
                init_half = jnp.sum(dhid, axis=0) * share

        media_grad = media_part
        rows = patches // 2
        own = lax.dynamic_slice_in_dim(media_part, odd * rows, rows, 1)
        rest = lax.dynamic_slice_in_dim(media_part, (1 - odd) * rows, rows, 1)
        media_grad = turn(head_fill(head_sum_half(jnp.concatenate([own, rest], 1))), 1)

        stats = jnp.stack([r for rr in gain_rows for r in rr] + [r for rr in bias_rows for r in rr])
        stats = jnp.pad(stats, ((0, -stats.shape[0] % 8), (0, 0)))
        stats = stats + swap(stats, "head", 1)
        init = init_part[:half] + swap(init_part[half:], "head", 1) + init_half
        pack = jnp.concatenate([init, stats], 0)
        for bit in head_bits[1:]:
            pack = pack + swap(pack, "head", bit)
        for bit in [1] + img_bits:
            pack = pack + swap(pack, "img", bit)
        init = turn(jnp.concatenate([pack[:half], swap(pack[:half], "head", 1)], 0), 0)
        count = layers * 3
        grad_gain = pack[half : half + count].reshape(layers, 3, width)
        grad_bias = pack[half + count : half + 2 * count].reshape(layers, 3, width)

        def piece(j):
            return jnp.stack([g[:, j * local : (j + 1) * local] for g in attn_grads])

        return (
            latents_out,
            media_grad,
            init,
            piece(0),
            piece(1),
            piece(2),
            jnp.stack([g[:, 3 * local :].T for g in attn_grads]),
            jnp.stack(up_grads),
            jnp.stack(down_grads),
            grad_gain,
            grad_bias,
        )

    return body


VM = pl.BlockSpec(memory_space=pltpu.VMEM)
SM = pl.BlockSpec(memory_space=pltpu.SMEM)
MIB = 1 << 20


def dot(a, b, ca=1, cb=0):
    return lax.dot_general(a, b, (((ca,), (cb,)), ((), ())), preferred_element_type=F32)


def zhat_of(x):
    center = x - jnp.mean(x, axis=-1, keepdims=True)
    rstd = lax.rsqrt(jnp.mean(center * center, axis=-1, keepdims=True) + 1e-05)
    return center * rstd, rstd


def phi_parts(u):
    cdf = 0.5 * (1.0 + lax.erf(u * 0.7071067811865476))
    pdf = jnp.exp(-0.5 * u * u) * 0.3989422804014327
    return cdf, pdf


def call(kernel, name, scalars, ins, outs, cost, vmem=24 * MIB, scratch=()):
    flops, moved = cost
    return pl.pallas_call(
        kernel,
        name=name,
        out_shape=[jax.ShapeDtypeStruct(s, d) for s, d in outs],
        in_specs=[SM] * len(scalars) + [VM] * len(ins),
        out_specs=[VM] * len(outs),
        scratch_shapes=scratch,
        compiler_params=pltpu.CompilerParams(vmem_limit_bytes=vmem),
        cost_estimate=pl.CostEstimate(flops=int(flops), bytes_accessed=int(moved), transcendentals=0),
    )(*scalars, *ins)


def media_kernel(media, gain, bias, wk, wv, mn_out, kp_out, vp_out):
    images, patches, width = media.shape
    for i in range(images):
        z, _ = zhat_of(media[i].astype(F32))
        mn = (z * gain[...] + bias[...]).astype(BF16)
        mn_out[i] = mn
        kp_out[i] = dot(mn, wk[...]).astype(BF16)
        vp_out[i] = dot(mn, wv[...]).astype(BF16)


def attn_fwd_kernel(
    counts, z_own, z_oth, gain, bias, wq, wk, wv, wo, kp, vp,
    part_own, part_oth, xn_out, q_out, kl_out, vl_out, o_out, pp_out, pl_out, *, first
):
    n, patches, local = kp.shape
    half = z_own.shape[1]
    rows = 2 * half
    shared = z_own.shape[0]
    for i in range(shared):
        z = jnp.concatenate([z_own[i], z_oth[i]], axis=0)
        xn_out[i] = (z * gain[...] + bias[...]).astype(BF16)
    x = xn_out[...].reshape(shared * rows, xn_out.shape[2])
    q = dot(x, wq[...]).astype(BF16)
    kl = dot(x, wk[...]).astype(BF16)
    vl = dot(x, wv[...]).astype(BF16)
    q_out[...] = q.reshape(q_out.shape)
    kl_out[...] = kl.reshape(kl_out.shape)
    vl_out[...] = vl.reshape(vl_out.shape)
    scale = HEAD_DIM ** (-0.5)
    for i in range(n):
        j = min(i, shared - 1)
        count = counts[first + i]
        seen = lax.broadcasted_iota(jnp.int32, (rows, patches), 1) < count
        mixed = []
        for h in range(local // HEAD_DIM):
            cols = slice(h * HEAD_DIM, (h + 1) * HEAD_DIM)
            qh = q[j * rows : (j + 1) * rows, cols]
            sp = dot(qh, kp[i, :, cols], 1, 1) * scale
            sp = jnp.where(seen, sp, -1e30)
            sl = dot(qh, kl[j * rows : (j + 1) * rows, cols], 1, 1) * scale
            top = jnp.maximum(
                jnp.max(sp, axis=-1, keepdims=True), jnp.max(sl, axis=-1, keepdims=True)
            )
            ep = jnp.exp(sp - top)
            el = jnp.exp(sl - top)
            den = jnp.sum(ep, axis=-1, keepdims=True) + jnp.sum(el, axis=-1, keepdims=True)
            ep = ep / den
            el = el / den
            pp_out[i, h] = ep
            pl_out[i, h] = el
            mixed.append(
                dot(ep.astype(BF16), vp[i, :, cols])
                + dot(el.astype(BF16), vl[j * rows : (j + 1) * rows, cols])
            )
        o_out[i] = jnp.concatenate(mixed, axis=1).astype(BF16)
    part = dot(o_out[...].reshape(n * rows, local), wo[...])
    for i in range(n):
        part_own[i] = part[i * rows : i * rows + half]
        part_oth[i] = part[i * rows + half : (i + 1) * rows]


def attn_bwd_kernel(
    dh_own, dh_oth, q, kl, vl, kp, vp, pp, p_l, wq, wk, wv, wo,
    dl_own, dl_oth, da_out, dq_out, dkl_out, dvl_out, dkp_out, dvp_out,
):
    n, patches, local = kp.shape
    half = dh_own.shape[1]
    rows = 2 * half
    shared = q.shape[0]
    width = dh_own.shape[2]
    scale = HEAD_DIM ** (-0.5)
    for i in range(n):
        da_out[i] = jnp.concatenate([dh_own[i], dh_oth[i]], axis=0).astype(BF16)
    dmix = dot(da_out[...].reshape(n * rows, width), wo[...], 1, 1).astype(BF16)
    for i in range(n):
        j = min(i, shared - 1)
        dqs, dkls, dvls, dkps, dvps = [], [], [], [], []
        for h in range(local // HEAD_DIM):
            cols = slice(h * HEAD_DIM, (h + 1) * HEAD_DIM)
            do = dmix[i * rows : (i + 1) * rows, cols]
            ep = pp[i, h]
            el = p_l[i, h]
            qh = q[j, :, cols]
            klh = kl[j, :, cols]
            kph = kp[i, :, cols]
            dpp = dot(do, vp[i, :, cols], 1, 1)
            dpl = dot(do, vl[j, :, cols], 1, 1)
            dvps.append(dot(ep.astype(BF16), do, 0, 0))
            dvls.append(dot(el.astype(BF16), do, 0, 0))
            total = jnp.sum(dpp * ep, axis=-1, keepdims=True) + jnp.sum(
                dpl * el, axis=-1, keepdims=True
            )
            dsp = (ep * (dpp - total)).astype(BF16)
            dsl = (el * (dpl - total)).astype(BF16)
            dqs.append((dot(dsp, kph) + dot(dsl, klh)) * scale)
            dkps.append(dot(dsp, qh, 0, 0) * scale)
            dkls.append(dot(dsl, qh, 0, 0) * scale)
        dq_out[i] = jnp.concatenate(dqs, axis=1).astype(BF16)
        dkl_out[i] = jnp.concatenate(dkls, axis=1).astype(BF16)
        dvl_out[i] = jnp.concatenate(dvls, axis=1).astype(BF16)
        dkp_out[i] = jnp.concatenate(dkps, axis=1).astype(BF16)
        dvp_out[i] = jnp.concatenate(dvps, axis=1).astype(BF16)
    dlat = (
        dot(dq_out[...].reshape(n * rows, local), wq[...], 1, 1)
        + dot(dkl_out[...].reshape(n * rows, local), wk[...], 1, 1)
        + dot(dvl_out[...].reshape(n * rows, local), wv[...], 1, 1)
    )
    for i in range(n):
        dl_own[i] = dlat[i * rows : i * rows + half]
        dl_oth[i] = dlat[i * rows + half : (i + 1) * rows]


def media_bwd_kernel(place, dkp, dvp, wk, wv, media, gain, *rest, add):
    olds, (m_own, m_oth, stats) = rest[: 2 if add else 0], rest[2 if add else 0 :]
    n, patches, local = dkp.shape
    half = patches // 2
    odd = place[0]
    sums = [0.0, 0.0]
    for i in range(n):
        for k, out in enumerate((m_own, m_oth)):
            start = pl.multiple_of(((odd + k) % 2) * half, half)
            d = dot(dkp[i, pl.ds(start, half), :], wk[...], 1, 1) + dot(
                dvp[i, pl.ds(start, half), :], wv[...], 1, 1
            )
            z, rstd = zhat_of(media[i, pl.ds(start, half), :].astype(F32))
            sums[0] = sums[0] + jnp.sum(d * z, axis=0, keepdims=True)
            sums[1] = sums[1] + jnp.sum(d, axis=0, keepdims=True)
            back = norm_back(d, z, rstd, gain[...])
            out[i] = back + olds[k][i] if add else back
    stats[0:1, :] = sums[0]
    stats[1:2, :] = sums[1]


def row_fwd_kernel(a, b, base, x_out, z_out):
    x = a[...] + b[...] + base[...]
    x_out[...] = x
    z_out[...] = zhat_of(x)[0]


def row_add_kernel(a, b, base, x_out):
    x_out[...] = a[...] + b[...] + base[...]


def row_bwd_kernel(a, b, base, x, gain, out, stats, *, share):
    d = a[...] + b[...]
    z, rstd = zhat_of(x[...])
    out[...] = base[...] + norm_back(d, z, rstd, gain[...])
    stats[0:1, :] = jnp.sum(d * z, axis=(0, 1), keepdims=True)[0] * share
    stats[1:2, :] = jnp.sum(d, axis=(0, 1), keepdims=True)[0] * share


def normed_rows(z_own, z_oth, gain, bias):
    n, half, width = z_own.shape
    z = jnp.concatenate([z_own[...], z_oth[...]], axis=1).reshape(n * 2 * half, width)
    return (z * gain[...] + bias[...]).astype(BF16)


def put_halves(part, own, oth):
    n, half, _ = own.shape
    for i in range(n):
        own[i] = part[2 * i * half : (2 * i + 1) * half]
        oth[i] = part[(2 * i + 1) * half : (2 * i + 2) * half]


def ffn_fwd_kernel(z_own, z_oth, gain, bias, up, down, part_own, part_oth):
    u = dot(normed_rows(z_own, z_oth, gain, bias), up[...])
    cdf, _ = phi_parts(u)
    put_halves(dot((u * cdf).astype(BF16), down[...]), part_own, part_oth)


def ffn_bwd_kernel(z_own, z_oth, gain, bias, dy_own, dy_oth, up, down, part_own, part_oth):
    n, half, width = z_own.shape
    u = dot(normed_rows(z_own, z_oth, gain, bias), up[...])
    dy = jnp.concatenate([dy_own[...], dy_oth[...]], axis=1).reshape(n * 2 * half, width)
    da = dot(dy.astype(BF16), down[...], 1, 1)
    cdf, pdf = phi_parts(u)
    du = (da * (cdf + u * pdf)).astype(BF16)
    put_halves(dot(du, up[...], 1, 1), part_own, part_oth)


def dw_attn_kernel(place, mn, xn, dq, dkl, dvl, dkp, dvp, o, da, own, oth):
    core = place[1]
    images, patches, width = mn.shape
    rows = xn.shape[1]
    local = dq.shape[2]
    half = width // 2
    dlat = jnp.concatenate([dq[...], dkl[...], dvl[...]], axis=2).reshape(images * rows, 3 * local)
    dpat = jnp.concatenate([dkp[...], dvp[...]], axis=2).reshape(images * patches, 2 * local)
    omix = o[...].reshape(images * rows, local)
    for k, out in enumerate((own, oth)):
        cols = pl.ds(pl.multiple_of(((core + k) % 2) * half, half), half)
        lat = 0.0
        for i in range(images):
            j = min(i, xn.shape[0] - 1)
            lat = lat + dot(xn[j, :, cols], dlat[i * rows : (i + 1) * rows], 0, 0)
        pat = dot(mn[:, :, cols].reshape(images * patches, half), dpat, 0, 0)
        out[:, :local] = lat[:, :local]
        out[:, local : 3 * local] = lat[:, local:] + pat
        two = dot(omix, da[:, :, cols].reshape(images * rows, half), 0, 0)
        for c in range(half // local):
            out[c * local : (c + 1) * local, 3 * local :] = two[:, c * local : (c + 1) * local]


def prep_kernel(*refs, pieces):
    zs, dys = refs[:pieces], refs[pieces : 2 * pieces]
    gain, bias, hn_out, hnt_out, dy_out = refs[2 * pieces :]
    start = 0
    for z, dy in zip(zs, dys):
        size = z.shape[0]
        hn = (z[...] * gain[...] + bias[...]).astype(BF16)
        hn_out[start : start + size] = hn
        hnt_out[:, start : start + size] = hn.T
        dy_out[start : start + size] = dy[...].astype(BF16)
        start += size


def dw_ffn_kernel(hn, hnt, dy, up, down, *rest):
    dup_out, ddown_out = rest[-2:]
    u = dot(hn[...], up[...])
    da = dot(dy[...], down[...], 1, 1)
    cdf, pdf = phi_parts(u)
    dup_out[...] = dot(hnt[...], (da * (cdf + u * pdf)).astype(BF16))
    ddown_out[...] = dot((u * cdf).astype(BF16), dy[...], 0, 0)


def sums_kernel(*refs, streams, share):
    it = iter(refs)

    def take(k):
        return [next(it) for _ in range(k)]

    dl_own, dl_oth, dhid = take(streams), take(streams), take(streams)
    (z_own, z_oth, x_own, x_oth, gain) = take(5)
    stats = [[take(streams) for _ in range(3)] for _ in range(2)]
    keep, send = take(2)
    half = z_own.shape[1]
    keep[...] = jnp.zeros_like(keep)
    send[...] = jnp.zeros_like(send)
    latent_gain = 0.0
    latent_bias = 0.0
    for group, z_ref, x_ref, out in ((dl_own, z_own, x_own, keep), (dl_oth, z_oth, x_oth, send)):
        z, rstd = z_ref[0], zhat_of(x_ref[0])[1]
        total = 0.0
        for ref in group:
            for i in range(ref.shape[0]):
                total = total + ref[i]
        latent_gain = latent_gain + jnp.sum(total * z, axis=0, keepdims=True)
        latent_bias = latent_bias + jnp.sum(total, axis=0, keepdims=True)
        back = norm_back(total, z, rstd, gain[...])
        if out is keep:
            extra = 0.0
            for ref in dhid:
                for i in range(ref.shape[0]):
                    extra = extra + ref[i]
            back = back + extra * share
        out[0:half] = back
    row = half
    for which in range(2):
        for layer in range(2):
            for norm in range(3):
                if layer == 0 and norm == 1:
                    value = latent_gain if which == 0 else latent_bias
                else:
                    value = 0.0
                    for ref in stats[layer][norm]:
                        value = value + ref[which : which + 1, :]
                keep[row : row + 1, :] = value
                send[row : row + 1, :] = value
                row += 1


def start_kernel(place, init, cot, z_own, z_oth, x_own, x_oth, *cots):
    odd = place[0]
    half = init.shape[0] // 2
    streams = len(cots) // 2
    n = cot.shape[0] // streams
    for k, (z_out, x_out) in enumerate(((z_own, x_own), (z_oth, x_oth))):
        rows = pl.ds(pl.multiple_of(((odd + k) % 2) * half, half), half)
        x = init[rows, :].astype(F32)
        x_out[0] = x
        z_out[0] = zhat_of(x)[0]
        for s in range(streams):
            for i in range(n):
                cots[2 * s + k][i] = cot[s * n + i, rows, :].astype(F32)


def split_kernel(place, *refs, parts):
    ins, outs = refs[: len(refs) - 2 * len(parts)], refs[len(refs) - 2 * len(parts) :]
    for k, (source, base, size, slot) in enumerate(parts):
        a, b = ins[2 * source], ins[2 * source + 1]
        half = size // 2
        bit = place[slot]
        for turn, out in ((bit, outs[2 * k]), (1 - bit, outs[2 * k + 1])):
            rows = pl.ds(pl.multiple_of(base + turn * half, half), half)
            out[...] = a[rows, :] + b[rows, :]


def grads_out_kernel(place, *refs, table, olds):
    outs = refs[-4:]
    ins = refs[: len(refs) - 4 - olds]
    local = outs[0].shape[2]
    for ref, start, size, base, terms in table:
        at = base
        for slot, flip, step in terms:
            at = at + ((place[slot] + flip) % 2) * step
        rows = pl.ds(pl.multiple_of(at, size), size)
        block = ins[ref][start : start + size, :]
        for j in range(3):
            outs[j][0, rows, :] = block[:, j * local : (j + 1) * local]
        across = pl.ds(pl.multiple_of((at // local) * local, local), local)
        down = pl.ds(pl.multiple_of(at % local, size), size)
        outs[3][0, down, across] = block[:, 3 * local :]


def rows_out_kernel(place, *refs):
    out = refs[-1]
    pieces = refs[:-1]
    streams = len(pieces) // 2
    n = out.shape[0] // streams
    half = out.shape[1] // 2
    odd = place[0]
    for s in range(streams):
        for k in range(2):
            rows = pl.ds(pl.multiple_of(((odd + k) % 2) * half, half), half)
            for i in range(n):
                out[s * n + i, rows, :] = pieces[2 * s + k][i].astype(out.dtype)


STREAMS = 2


def make_fast_body(heads_size, img_size):
    head_bits = [1 << k for k in range(heads_size.bit_length() - 1)]
    img_bits = [1 << k for k in range(1, img_size.bit_length() - 1)]
    share = 2.0 / heads_size

    def swap(x, axis, bit):
        size = heads_size if axis == "head" else img_size
        return lax.ppermute(x, axis, [(i, i ^ bit) for i in range(size)])

    def body(
        latent_init,
        media,
        patch_counts,
        query_weight,
        key_weight,
        value_weight,
        w_out,
        up_weight,
        w_down,
        ln_gain,
        ln_bias,
        latent_cot,
    ):
        images, patches, width = media.shape
        latents = latent_init.shape[0]
        layers = query_weight.shape[0]
        local = query_weight.shape[2]
        ff = up_weight.shape[2]
        heads = local // HEAD_DIM
        half = latents // 2
        streams = STREAMS
        n = images // streams
        rows_n = n * latents
        head_at = lax.axis_index("head")
        img_at = lax.axis_index("img")
        place = jnp.stack(
            [head_at % 2, img_at % 2] + [(img_at // bit) % 2 for bit in img_bits]
        ).astype(jnp.int32)
        slot_of = {bit: 2 + k for k, bit in enumerate(img_bits)}
        half_rows = ((n, half, width), F32)
        wq = [query_weight[k] for k in range(layers)]
        wk = [key_weight[k] for k in range(layers)]
        wv = [value_weight[k] for k in range(layers)]
        wo = [w_out[k] for k in range(layers)]
        up = [up_weight[k] for k in range(layers)]
        down = [w_down[k] for k in range(layers)]
        gain = [[ln_gain[k, j : j + 1] for j in range(3)] for k in range(layers)]
        bias = [[ln_bias[k, j : j + 1] for j in range(3)] for k in range(layers)]
        media_s = [media[s * n : (s + 1) * n] for s in range(streams)]

        def head_pair(own, oth):
            kept = own + swap(oth, "head", 1)
            for bit in head_bits[1:-1]:
                kept = kept + swap(kept, "head", bit)
            return kept, swap(kept, "head", head_bits[-1])

        def start():
            outs = [((1, half, width), F32)] * 4 + [half_rows] * (2 * streams)
            got = call(
                start_kernel, "start", [place], [latent_init, latent_cot], outs, (1e6, 1e6)
            )
            return got[:4], [(got[4 + 2 * s], got[5 + 2 * s]) for s in range(streams)]

        (z0_own, z0_oth, x0_own, x0_oth), cots = start()

        def media_part(layer):
            kv = ((images, patches, local), BF16)
            return call(
                media_kernel,
                "media_%d" % layer,
                [],
                [media, gain[layer][0], bias[layer][0], wk[layer], wv[layer]],
                [((images, patches, width), BF16), kv, kv],
                (4 * images * patches * width * local, 4e6),
            )

        mn, kps, vps = zip(*[media_part(layer) for layer in range(layers)])

        def attn_fwd(layer, s, z):
            m = z[0].shape[0]
            outs = [half_rows, half_rows, ((m, latents, width), BF16)]
            outs += [((m, latents, local), BF16)] * 3 + [((n, latents, local), BF16)]
            outs += [((n, heads, latents, patches), F32), ((n, heads, latents, latents), F32)]
            at = slice(s * n, (s + 1) * n)
            got = call(
                lambda *r: attn_fwd_kernel(*r, first=s * n),
                "attn_fwd_%d_%d" % (layer, s),
                [patch_counts],
                [z[0], z[1], gain[layer][1], bias[layer][1], wq[layer], wk[layer], wv[layer],
                 wo[layer], kps[layer][at], vps[layer][at]],
                outs,
                (2 * rows_n * width * local * 4, 4e6),
            )
            names = ("xn", "q", "kl", "vl", "o", "pp", "p_l")
            return got[0], got[1], dict(zip(names, got[2:]))

        def row_fwd(a, b, base, name):
            return call(
                row_fwd_kernel, name, [], [a, b, base], [half_rows, half_rows], (1e6, 1e6)
            )

        def row_bwd(a, b, base, x, gains, name):
            return call(
                lambda *r: row_bwd_kernel(*r, share=share),
                name, [], [a, b, base, x, gains],
                [half_rows, ((2, width), F32)], (1e6, 1e6),
            )

        def ffn_fwd(layer, s, z):
            return call(
                ffn_fwd_kernel, "ffn_fwd_%d_%d" % (layer, s), [],
                [z[0], z[1], gain[layer][2], bias[layer][2], up[layer], down[layer]],
                [half_rows, half_rows], (4 * rows_n * width * ff, 6e6),
            )

        def ffn_bwd(layer, s, z, dy):
            return call(
                ffn_bwd_kernel, "ffn_bwd_%d_%d" % (layer, s), [],
                [z[0], z[1], gain[layer][2], bias[layer][2], dy[0], dy[1], up[layer], down[layer]],
                [half_rows, half_rows], (6 * rows_n * width * ff, 6e6),
            )

        def attn_bwd(layer, s, dh, c):
            at = slice(s * n, (s + 1) * n)
            lat = ((n, latents, local), BF16)
            pat = ((n, patches, local), BF16)
            got = call(
                attn_bwd_kernel, "attn_bwd_%d_%d" % (layer, s), [],
                [dh[0], dh[1], c["q"], c["kl"], c["vl"], kps[layer][at], vps[layer][at], c["pp"],
                 c["p_l"], wq[layer], wk[layer], wv[layer], wo[layer]],
                [half_rows, half_rows, ((n, latents, width), BF16), lat, lat, lat, pat, pat],
                (2 * rows_n * width * local * 4, 4e6),
            )
            return got[0], got[1], dict(zip(("da", "dq", "dkl", "dvl", "dkp", "dvp"), got[2:]))

        def media_bwd(layer, s, d, old):
            part = ((n, patches // 2, width), F32)
            return call(
                lambda *r: media_bwd_kernel(*r, add=old is not None),
                "media_bwd_%d_%d" % (layer, s), [place],
                [d["dkp"], d["dvp"], wk[layer], wv[layer], media_s[s], gain[layer][0]]
                + ([] if old is None else list(old)),
                [part, part, ((2, width), F32)],
                (4 * n * patches * width * local, 6e6),
            )

        def joined(pieces):
            return pieces[0] if len(pieces) == 1 else jnp.concatenate(pieces, 0)

        def img_gather(one, two):
            order = (img_bits, img_bits[::-1])
            lists = [[one], [two]]
            for step in range(len(img_bits)):
                for k in range(2):
                    have = joined(lists[k])
                    lists[k] = [have, swap(have, "img", order[k][step])]
            mine = lists[0] + lists[1]
            other = [swap(x, "img", 1) for x in mine]
            cut = len(lists[0])
            return mine[:cut] + other[:cut], mine[cut:] + other[cut:]

        def img_sum(own, oth):
            other = swap(oth, "img", 1)
            size = own.shape[0] // 2
            order = (img_bits, img_bits[::-1])
            parts = ((0, 0, size, slot_of[order[0][0]]), (0, size, size, slot_of[order[1][0]]))
            ins = [own, other]
            for step in range(len(img_bits)):
                if step:
                    parts = tuple((k, 0, size, slot_of[order[k][step]]) for k in range(2))
                size //= 2
                got = call(
                    lambda *r, parts=parts: split_kernel(*r, parts=parts),
                    "split_%d" % step, [place], ins,
                    [((size, own.shape[1]), F32)] * 4, (1e6, 4e6),
                )
                ins = []
                for k in range(2):
                    ins += [got[2 * k], swap(got[2 * k + 1], "img", order[k][step])]
            lists = [[ins[0] + ins[1]], [ins[2] + ins[3]]]
            for step in reversed(range(len(img_bits))):
                for k in range(2):
                    have = joined(lists[k])
                    lists[k] = [have, swap(have, "img", order[k][step])]
            mine = lists[0] + lists[1]
            full = own.shape[0]
            table = []
            for core in range(2):
                ref = core * len(mine)
                for k in range(2):
                    for index in range(1 << len(img_bits)):
                        terms = [(1, core, full)]
                        step = full // 2
                        for depth, bit in enumerate(order[k]):
                            step //= 2
                            flip = (index >> (len(img_bits) - 1 - depth)) & 1
                            terms.append((slot_of[bit], flip, step))
                        per = mine[2 * k].shape[0] // size
                        table.append(
                            (ref + 2 * k + index // per, (index % per) * size, size,
                             k * (full // 2), tuple(terms))
                        )
            return mine + [swap(x, "img", 1) for x in mine], table

        def grads_out(layer, pieces, table, old):
            outs = [(layers, width, local)] * 3 + [(layers, local, width)]
            count = 1 + len(pieces)
            return pl.pallas_call(
                lambda *r: grads_out_kernel(*r, table=table, olds=0 if old is None else 4),
                name="grads_out_%d" % layer,
                grid=(1,),
                out_shape=[jax.ShapeDtypeStruct(s, F32) for s in outs],
                in_specs=[SM] + [VM] * len(pieces)
                + [pl.BlockSpec(memory_space=pl.ANY)] * (0 if old is None else 4),
                out_specs=[pl.BlockSpec((1,) + s[1:], lambda i: (layer, 0, 0)) for s in outs],
                input_output_aliases={} if old is None else {count + k: k for k in range(4)},
                compiler_params=pltpu.CompilerParams(vmem_limit_bytes=24 * MIB),
                cost_estimate=pl.CostEstimate(
                    flops=0, bytes_accessed=8 * width * local * 4, transcendentals=0
                ),
            )(place, *pieces, *([] if old is None else old))

        chunks = 4 if ff % 512 == 0 else 1
        block = ff // chunks

        def ffn_grads(layer, zs, dys, old):
            total = sum(z.shape[0] for z in zs)
            wide = ((total, width), BF16)
            hn, hnt, dy = call(
                lambda *r: prep_kernel(*r, pieces=len(zs)),
                "prep_%d" % layer, [], zs + dys + [gain[layer][2], bias[layer][2]],
                [wide, ((width, total), BF16), wide], (1e6, 14e6), vmem=32 * MIB,
            )
            for c in range(chunks):
                have = old is not None
                old = pl.pallas_call(
                    dw_ffn_kernel,
                    name="dw_ffn_%d_%d" % (layer, c),
                    grid=(1,),
                    out_shape=[
                        jax.ShapeDtypeStruct((layers, width, ff), F32),
                        jax.ShapeDtypeStruct((layers, ff, width), F32),
                    ],
                    in_specs=[VM, VM, VM]
                    + [
                        pl.BlockSpec((None, width, block), lambda i, c=c: (layer, 0, c)),
                        pl.BlockSpec((None, block, width), lambda i, c=c: (layer, c, 0)),
                    ]
                    + ([pl.BlockSpec(memory_space=pl.ANY)] * 2 if have else []),
                    out_specs=[
                        pl.BlockSpec((None, width, block), lambda i, c=c: (layer, 0, c)),
                        pl.BlockSpec((None, block, width), lambda i, c=c: (layer, c, 0)),
                    ],
                    input_output_aliases={5: 0, 6: 1} if have else {},
                    compiler_params=pltpu.CompilerParams(vmem_limit_bytes=24 * MIB),
                    cost_estimate=pl.CostEstimate(
                        flops=8 * total * width * block, bytes_accessed=8 * width * block,
                        transcendentals=0,
                    ),
                )(hn, hnt, dy, up_weight, w_down, *(old if have else ()))
            return old

        span = range(streams)
        x_in = [[None] * streams for _ in range(layers)]
        hid = [[None] * streams for _ in range(layers)]
        hid_z = [[None] * streams for _ in range(layers)]
        kept = [[None] * streams for _ in range(layers)]
        x_in[0] = [x0_own] * streams
        z = [(z0_own, z0_oth)] * streams
        for layer in range(layers):
            parts = [None] * streams
            for s in span:
                own, oth, kept[layer][s] = attn_fwd(layer, s, z[s])
                parts[s] = head_pair(own, oth)
            for s in span:
                hid[layer][s], zr = row_fwd(*parts[s], x_in[layer][s], "row_h_%d_%d" % (layer, s))
                hid_z[layer][s] = (zr, swap(zr, "head", 1))
            if layer + 1 == layers:
                break
            for s in span:
                parts[s] = head_pair(*ffn_fwd(layer, s, hid_z[layer][s]))
            for s in span:
                x_in[layer + 1][s], zr = row_fwd(
                    *parts[s], hid[layer][s], "row_x_%d_%d" % (layer, s)
                )
                z[s] = (zr, swap(zr, "head", 1))
        base = [cots[s][0] for s in span]
        dys = list(cots)
        stats = [[[None] * streams for _ in range(3)] for _ in range(layers)]
        media_parts = [None] * streams
        ffn_out = None
        attn_out = None
        gathered = None
        for layer in reversed(range(layers)):
            parts = [None] * streams
            dhid = [None] * streams
            dh = [None] * streams
            grads = [None] * streams
            for s in span:
                parts[s] = head_pair(*ffn_bwd(layer, s, hid_z[layer][s], dys[s]))
            if layer + 1 == layers:
                tail = [head_pair(*ffn_fwd(layer, s, hid_z[layer][s])) for s in span]
            for s in span:
                dhid[s], stats[layer][2][s] = row_bwd(
                    *parts[s], base[s], hid[layer][s], gain[layer][2], "row_b_%d_%d" % (layer, s)
                )
                dh[s] = (dhid[s], swap(dhid[s], "head", 1))
            flat = lambda pair: joined([p.reshape(n * half, width) for p in pair])
            z_parts = [flat(hid_z[layer][s]) for s in span]
            d_parts = [flat(dys[s]) for s in span]
            if streams == 1:
                z_parts = list(jnp.split(z_parts[0], 2, 0))
                d_parts = list(jnp.split(d_parts[0], 2, 0))
            za, zb = img_gather(*z_parts)
            da, db = img_gather(*d_parts)
            ffn_out = ffn_grads(layer, za + zb, da + db, ffn_out)
            parts = [None] * streams
            for s in span:
                own, oth, grads[s] = attn_bwd(layer, s, dh[s], kept[layer][s])
                parts[s] = (own, oth)
                if layer > 0:
                    parts[s] = head_pair(own, oth)
            if layer > 0:
                for s in span:
                    base[s], stats[layer][1][s] = row_bwd(
                        *parts[s], dhid[s], x_in[layer][s], gain[layer][1],
                        "row_g_%d_%d" % (layer, s),
                    )
                    dys[s] = (base[s], swap(base[s], "head", 1))
            for s in span:
                own, oth, stats[layer][0][s] = media_bwd(layer, s, grads[s], media_parts[s])
                media_parts[s] = (own, oth)

            def cat(key, source):
                return joined([source[s][key] for s in span])

            xn = kept[layer][0]["xn"] if layer == 0 else cat("xn", kept[layer])
            own, oth = call(
                dw_attn_kernel, "dw_attn_%d" % layer, [place],
                [mn[layer], xn, cat("dq", grads), cat("dkl", grads), cat("dvl", grads),
                 cat("dkp", grads), cat("dvp", grads), cat("o", kept[layer]), cat("da", grads)],
                [((width // 2, 4 * local), F32)] * 2,
                (8 * images * patches * width * local, 8e6),
            )
            pieces, table = img_sum(own, oth)
            attn_out = grads_out(layer, pieces, table, attn_out)

        media_rows = []
        for s in span:
            kept_rows, other = head_pair(*media_parts[s])
            rows = kept_rows + other
            media_rows += [rows, swap(rows, "head", 1)]
        media_grad = pl.pallas_call(
            rows_out_kernel, name="media_out",
            out_shape=jax.ShapeDtypeStruct((images, patches, width), F32),
            in_specs=[SM] + [VM] * len(media_rows),
            out_specs=pl.BlockSpec(),
            compiler_params=pltpu.CompilerParams(vmem_limit_bytes=24 * MIB),
        )(place, *media_rows)
        out_rows = []
        for s in span:
            x_out, = call(
                row_add_kernel, "row_o_%d" % s, [], [*tail[s], hid[layers - 1][s]], [half_rows],
                (1e6, 1e6),
            )
            out_rows += [x_out, swap(x_out, "head", 1)]
        latents_out = pl.pallas_call(
            rows_out_kernel, name="latents_out",
            out_shape=jax.ShapeDtypeStruct((images, latents, width), BF16),
            in_specs=[SM] + [VM] * len(out_rows),
            out_specs=pl.BlockSpec(),
            compiler_params=pltpu.CompilerParams(vmem_limit_bytes=24 * MIB),
        )(place, *out_rows)

        total = half + -(-4 * layers * 3 // 16) * 8
        small = [r for norm in stats for group in norm for r in group if r is not None]
        keep, send = call(
            lambda *r: sums_kernel(*r, streams=streams, share=share), "sums", [],
            [p[0] for p in parts] + [p[1] for p in parts] + dhid
            + [z0_own, z0_oth, x0_own, x0_oth, gain[0][1]]
            + [r for layer in range(layers) for k in range(3)
               for r in (stats[layer][k] if (layer, k) != (0, 1) else stats[0][2])],
            [((total, width), F32)] * 2, (1e6, 1e6),
        )
        pack = keep + swap(send, "head", 1)
        for bit in head_bits[1:]:
            pack = pack + swap(pack, "head", bit)
        for bit in [1] + img_bits:
            pack = pack + swap(pack, "img", bit)
        mine = pack[:half]
        other = swap(mine, "head", 1)
        init = jnp.where(
            head_at % 2 == 0,
            jnp.concatenate([mine, other], 0),
            jnp.concatenate([other, mine], 0),
        )
        count = layers * 3
        return (
            latents_out,
            media_grad,
            init,
            attn_out[0],
            attn_out[1],
            attn_out[2],
            attn_out[3],
            ffn_out[0],
            ffn_out[1],
            pack[half : half + count].reshape(layers, 3, width),
            pack[half + count : half + 2 * count].reshape(layers, 3, width),
        )

    return body


def fits(mesh):
    return mesh.shape["head"] <= 8 and mesh.shape["img"] <= 8


def solution(mesh):
    in_specs = (
        P(),
        P("img", None, None),
        P("img"),
        P(None, None, "head"),
        P(None, None, "head"),
        P(None, None, "head"),
        P(None, "head", None),
        P(None, None, "head"),
        P(None, "head", None),
        P(),
        P(),
        P("img", None, None),
    )
    out_specs = (
        P("img", None, None),
        P("img", None, None),
        P(),
        P(None, None, "head"),
        P(None, None, "head"),
        P(None, None, "head"),
        P(None, "head", None),
        P(None, None, "head"),
        P(None, "head", None),
        P(),
        P(),
    )
    make = make_fast_body if fits(mesh) else make_body
    return jax.shard_map(
        make(mesh.shape["head"], mesh.shape["img"]),
        mesh=mesh,
        in_specs=in_specs,
        out_specs=out_specs,
        check_vma=False,
    )
```
